32 devices in a mesh: section: 2 (over x), expert: 16 (over z, y, core).
Axes of the slice: x: 2, y: 2, z: 4, core: 2. Of those that a mesh axis runs over, the one named last changes fastest.
Arguments:
- carried: bfloat16 [2, 3072, 2048], P('section', 'expert'), may hold values from -6 to 6
- norm_gain: float32 [2, 2048], P('section'), may hold values from 0.25 to 1.75
- w_up: bfloat16 [2, 2048, 3072], P('section', None, 'expert'), may hold values from -0.125 to 0.125
- w_down: bfloat16 [2, 3072, 2048], P('section', 'expert'), may hold values from -0.21875 to 0.21875
- routes: int32 [1, 2, 3072, 2], P(None, 'section', 'expert'), may hold values from 0 to 3, all different within a row; in each aligned block of 192 rows (0 to 191, 192 to 383, ..., all dimensions but the last counted through in order) at most 120 rows name the same one
- gate_weights: float32 [1, 2, 3072, 2], P(None, 'section', 'expert'), may hold values from 0.3 to 1
Outputs:
- advanced: bfloat16 [2, 3072, 2048], P('section', 'expert')
The draws below stay inside these ranges and needn't reach their ends.
Inputs may be any that keep to these rules, and one draw needn't show every extreme that they name: `routes`: each token names two different experts. Among the 192 tokens of one device at one step and section, no expert is named more than 120 times, a bound that some block reaches.
All inputs are finite; a program needn't handle non-finite values.
Results may differ from the reference program's by a relative error of at most 0.0052.
Values may be sent and summed in bfloat16 or wider, within the bound.
No kernel may reach another device: no remote copies, remote signals or barrier semaphores. Data moves between devices by JAX's collectives and lax.ppermute only.
A program may use at most 64 MiB of HBM per device.

```python
import math
import jax
import jax.numpy as jnp
import numpy as np
from jax import lax

D = 2048
H = 768
TOK_DEV = 192
TICKS = 1
EXPERTS = 4
TOKENS = 3072
CAP = 120
N_SECTION = 2
N_EXPERT = 16


def block_scale(key, extent, shards, low, largest):
    loudness = 1.0
    for dim, blocks in shards:
        heights = jax.random.uniform(jax.random.fold_in(jax.random.fold_in(key, 6), dim), (blocks,), jnp.float32, low / len(shards), largest / len(shards))
        loudness = loudness * jnp.repeat(jnp.exp(heights), extent[dim] // blocks).reshape((-1,) + (1,) * (len(extent) - 1 - dim))
    return loudness


def assign_block(own_key, own, number, rows, count, top, bound, lean):
    ranking = jax.random.permutation(own_key, count)
    packed, ordinary = shares(count, rows * top, bound, lean, True), shares(count, rows * top, bound, lean, False)
    places = jnp.arange(count)

    def named(sizes, rotation):
        used = int((sizes > 0).sum())
        fixed = max(1, used // 4)
        shifted = fixed + (places - fixed + rotation * (used - fixed)) % max(1, count - fixed)
        return jnp.zeros((count,), jnp.int32).at[ranking[jnp.where(places < fixed, places, shifted)]].set(jnp.asarray(sizes, jnp.int32))

    sizes = jnp.where(number % 4 == 0, named(packed, number // 4), named(ordinary, number - number // 4 - 1))
    mixed = jax.random.permutation(jax.random.fold_in(own, 3), count)
    donor, sink = mixed[0:count // 2 * 2:2], mixed[1:count // 2 * 2:2]
    margin = jnp.minimum(sizes[donor] - 1, bound - sizes[sink]) // 2
    margin = jnp.where((donor == ranking[0]) | (sink == ranking[0]) | (sizes[sink] == 0), 0, jnp.maximum(margin, 0))
    shifted = jax.random.randint(jax.random.fold_in(own, 4), (count // 2,), 0, 1 << 20) % (margin + 1)
    sizes = sizes.at[donor].add(-shifted).at[sink].add(shifted)
    labels = jnp.searchsorted(jnp.cumsum(sizes), jnp.arange(rows * top), side="right").astype(jnp.int32)
    table = labels.reshape(top, rows).T
    table = table[jax.random.permutation(jax.random.fold_in(own, 1), rows)]
    rotation = jax.random.randint(jax.random.fold_in(own, 2), (rows, 1), 0, top)
    return jnp.take_along_axis(table, (jnp.arange(top)[None, :] + rotation) % top, axis=1)


def shares(number_of, total, most, lean, full):
    portions = [(1 << 20) // math.isqrt(rank ** lean) + 1 for rank in range(1, number_of + 1)]
    largest = most if full else min(most, max(-(-total // number_of), total * portions[0] // sum(portions)))
    least = 1 if total - largest >= number_of - 1 else 0
    given, rest = [largest] + [least] * (number_of - 1), total - largest - least * (number_of - 1)
    while rest > 0:
        candidates = [i for i in range(1, number_of) if given[i] < largest] or [i for i in range(1, number_of) if given[i] < most]
        whole, remaining = sum([portions[i] for i in candidates]), rest
        for i in candidates:
            addition = min(most - given[i], max(1, remaining * portions[i] // whole), rest)
            given[i] = given[i] + addition
            rest = rest - addition
    return np.array(given)


def scatter_about(key, extent, width, reach, shards=(), kind=jnp.bfloat16):
    entries = jax.random.normal(key, extent, jnp.float32) * width
    if len(shards) > 0:
        entries = block_scale(key, extent, shards, -0.22, 0.18) * entries
    return jnp.clip(entries, min=-reach, max=reach).astype(kind)


def setup_inputs(seed: int = 0) -> dict:
    splits = jax.random.split(jax.random.key(seed), 7)
    carried = scatter_about(splits[0], (N_SECTION, TOKENS, D), 1.0, 6.0, ((0, 2), (1, 16)))
    norm_gain = jnp.clip(1.0 + 0.15 * jax.random.normal(splits[1], (N_SECTION, D), jnp.float32), 0.25, 1.75)
    w_up = scatter_about(splits[2], (N_SECTION, D, EXPERTS * H), D ** -0.5, 0.125, ((0, 2), (2, 16)))
    w_down = scatter_about(splits[3], (N_SECTION, EXPERTS * H, D), H ** -0.5, 0.21875, ((0, 2), (1, 16)))
    routes_keys = jax.random.split(jax.random.fold_in(splits[4], 1), TICKS * N_SECTION * TOKENS // TOK_DEV)
    routes_turns = jax.random.permutation(jax.random.fold_in(splits[4], 3), TICKS * N_SECTION * TOKENS // TOK_DEV)
    routes = jax.vmap(lambda own, number: assign_block(jax.random.fold_in(splits[4], 2), own, number, TOK_DEV, EXPERTS, 2, CAP, 1))(routes_keys, routes_turns).reshape((TICKS, N_SECTION, TOKENS, 2))
    gate_weights = jnp.clip(0.3 + 0.7 * jax.random.uniform(splits[5], (TICKS, N_SECTION, TOKENS, 2), jnp.float32) ** block_scale(splits[5], (TICKS, N_SECTION, TOKENS, 2), ((1, 2), (2, 16)), -0.2, 0.2), 0.3, 1.0)
    return {"carried": carried, "norm_gain": norm_gain, "w_up": w_up, "w_down": w_down, "routes": routes, "gate_weights": gate_weights}


def half_output(row_block, up_part, down_part):
    hidden = jax.nn.gelu(jnp.dot(row_block, up_part, preferred_element_type=jnp.float32)).astype(jnp.bfloat16)
    return jnp.dot(hidden, down_part, preferred_element_type=jnp.float32).astype(jnp.bfloat16)

def section_layer(current, gain_row, up_section, down_section, expert_ids, weights_now):
    experts = N_EXPERT // 4
    capacity = min(TOK_DEV, 4 * ((5 * TOK_DEV + 8 * experts - 1) // (8 * experts)))
    half_width = H // 2
    per_expert = N_EXPERT * capacity
    values = current.astype(jnp.float32)
    inverse_rms = lax.rsqrt(lax.optimization_barrier(jnp.mean(values * values, axis=-1, keepdims=True)) + 1e-05)
    normed = (values * inverse_rms * gain_row).astype(jnp.bfloat16)
    flat_ids = expert_ids.reshape(N_EXPERT, TOK_DEV * 2)
    one_hot = (flat_ids[:, :, None] == jnp.arange(experts, dtype=jnp.int32)[None, None, :]).astype(jnp.int32)
    position = lax.optimization_barrier(jnp.sum((jnp.cumsum(one_hot, axis=1) - one_hot) * one_hot, axis=2))
    sources = jnp.arange(N_EXPERT, dtype=jnp.int32)[:, None]
    slot_keys = (flat_ids * per_expert + sources * capacity + position).reshape(-1).astype(jnp.int32)
    row_ids = jnp.arange(TOKENS * 2, dtype=jnp.int32) // 2
    slot_table = jnp.full((experts * per_expert,), TOKENS, jnp.int32).at[slot_keys].set(row_ids)
    slot_table = slot_table.reshape(experts, per_expert)
    padded = jnp.concatenate([normed, jnp.zeros((1, D), jnp.bfloat16)], axis=0)

    def one_expert(expert):
        row_block = padded[slot_table[expert]]
        total = jnp.zeros((per_expert, D), jnp.float32)
        for half in range(2):
            col_start = (expert * H + half * half_width).astype(jnp.int32)
            up_part = lax.dynamic_slice_in_dim(up_section, col_start, half_width, 1)
            down_part = lax.dynamic_slice_in_dim(down_section, col_start, half_width, 0)
            total = total + half_output(row_block, up_part, down_part).astype(jnp.float32)
        return total.astype(jnp.bfloat16)
    outputs = lax.map(one_expert, jnp.arange(experts, dtype=jnp.int32))
    gathered = outputs.reshape(-1, D)[slot_keys].astype(jnp.float32).reshape(TOKENS, 2, D)
    updated = values + weights_now[:, 0:1] * gathered[:, 0] + weights_now[:, 1:2] * gathered[:, 1]
    return updated.astype(jnp.bfloat16)

def reference(carried, norm_gain, w_up, w_down, routes, gate_weights):
    current = carried
    for tick_index in range(TICKS):

        def per_section(section_index):
            return section_layer(current[section_index], norm_gain[section_index], w_up[section_index], w_down[section_index], routes[tick_index, section_index], gate_weights[tick_index, section_index])
        updated = lax.map(per_section, jnp.arange(N_SECTION, dtype=jnp.int32))
        current = jnp.roll(updated, 1, axis=0)
    return current
```

```python
import functools

import jax
import jax.numpy as jnp
from jax import lax
from jax.experimental import pallas as pl
from jax.experimental.pallas import tpu as pltpu
from jax.sharding import PartitionSpec as P

VMEM = pl.BlockSpec(memory_space=pltpu.VMEM)
ANY = pl.BlockSpec(memory_space=pl.ANY)
BF16, F32 = jnp.bfloat16, jnp.float32


def exchanged(value, distance):
    count = lax.axis_size("expert")
    return lax.ppermute(value, "expert", [(i, i ^ distance) for i in range(count)])


def advanced(value, distance):
    sections, count = lax.axis_size("section"), lax.axis_size("expert")
    pairs = [
        (s * count + i, (s + 1) % sections * count + (i ^ distance))
        for s in range(sections)
        for i in range(count)
    ]
    return lax.ppermute(value, ("section", "expert"), pairs)


def dispatch_kernel(experts, capacity, x_ref, gain_ref, routes_ref, gates_ref, info_ref, *out_refs):
    rows = x_ref.shape[0]
    own = lax.axis_index("expert") // 4
    r0, r1 = routes_ref[0:1, :], routes_ref[1:2, :]
    padded = max(experts, 8)
    ids = lax.broadcasted_iota(jnp.int32, (padded, rows), 0)
    named = jnp.where((ids == r0) | (ids == r1), 1.0, 0.0)
    before = lax.broadcasted_iota(jnp.int32, (rows, rows), 0) < lax.broadcasted_iota(
        jnp.int32, (rows, rows), 1
    )
    place = jnp.dot(
        named.astype(BF16), jnp.where(before, 1.0, 0.0).astype(BF16), preferred_element_type=F32
    )
    p0 = jnp.sum(jnp.where(ids == r0, place, 0.0), axis=0, keepdims=True)
    p1 = jnp.sum(jnp.where(ids == r1, place, 0.0), axis=0, keepdims=True)
    t0 = (r0 ^ own) * capacity + p0.astype(jnp.int32)
    t1 = (r1 ^ own) * capacity + p1.astype(jnp.int32)
    info_ref[0:1, :] = t0.astype(F32)
    info_ref[1:2, :] = t1.astype(F32)
    info_ref[2:4, :] = gates_ref[...]
    info_ref[4:8, :] = jnp.zeros((4, rows), F32)
    slots = lax.broadcasted_iota(jnp.int32, (experts * capacity, rows), 0)
    chosen = jnp.where((slots == t0) | (slots == t1), 1.0, 0.0).astype(BF16)
    values = x_ref[...].astype(F32)
    scale = lax.rsqrt(jnp.mean(values * values, axis=-1, keepdims=True) + 1e-05)
    normed = (values * scale * gain_ref[...]).astype(BF16)
    sent = jnp.dot(chosen, normed, preferred_element_type=F32)
    for d, out_ref in enumerate(out_refs):
        out_ref[...] = sent[d * capacity : (d + 1) * capacity].astype(BF16)


def dispatch(x, gain, routes, gates, experts, capacity):
    rows, width = x.shape
    return pl.pallas_call(
        functools.partial(dispatch_kernel, experts, capacity),
        out_shape=[jax.ShapeDtypeStruct((8, rows), F32)]
        + [jax.ShapeDtypeStruct((capacity, width), BF16)] * experts,
        in_specs=[VMEM] * 4,
        out_specs=[VMEM] * (experts + 1),
        cost_estimate=pl.CostEstimate(
            flops=2 * experts * capacity * rows * width,
            bytes_accessed=2 * width * (rows + experts * capacity),
            transcendentals=0,
        ),
        name="dispatch",
    )(x, gain, routes, gates)


def ffn_kernel(groups, *refs):
    row_refs, refs = refs[:groups], refs[groups:]
    up_refs, down_refs, refs = refs[:4], refs[4:8], refs[8:]
    out_refs, (up, down, sems) = refs[:groups], refs[groups:]
    quarter = up_refs[0].shape[0]
    copies = [
        pltpu.make_async_copy(src, dst.at[pl.ds(i * quarter, quarter)], sems.at[k, i])
        for k, (sources, dst) in enumerate(((up_refs, up), (down_refs, down)))
        for i, src in enumerate(sources)
    ]
    for copy in copies:
        copy.start()
    rows = jnp.concatenate([ref[...].astype(F32) for ref in row_refs], axis=0).astype(BF16)
    for copy in copies[:4]:
        copy.wait()
    hidden = lax.dot_general(
        rows, up[...], (((1,), (1,)), ((), ())), preferred_element_type=F32
    )
    hidden = jax.nn.gelu(hidden).astype(BF16)
    for copy in copies[4:]:
        copy.wait()
    out = jnp.dot(hidden, down[...], preferred_element_type=F32)
    capacity = out_refs[0].shape[0]
    for d, out_ref in enumerate(out_refs):
        out_ref[...] = out[d * capacity : (d + 1) * capacity].astype(BF16)


def ffn(rows, ups, downs):
    groups, (capacity, width) = len(rows), rows[0].shape
    quarter = ups[0].shape[0]
    return pl.pallas_call(
        functools.partial(ffn_kernel, groups),
        out_shape=[jax.ShapeDtypeStruct((capacity, width), BF16)] * groups,
        in_specs=[VMEM] * groups + [ANY] * 8,
        out_specs=[VMEM] * groups,
        scratch_shapes=[
            pltpu.VMEM((4 * quarter, width), BF16),
            pltpu.VMEM((4 * quarter, width), BF16),
            pltpu.SemaphoreType.DMA((2, 4)),
        ],
        cost_estimate=pl.CostEstimate(
            flops=16 * groups * capacity * quarter * width,
            bytes_accessed=4 * width * (groups * capacity + 4 * quarter),
            transcendentals=4 * groups * capacity * quarter,
        ),
        name="ffn",
    )(*rows, *ups, *downs)


def combine_kernel(x_ref, info_ref, *refs):
    result_refs, out_ref = refs[:-1], refs[-1]
    rows = x_ref.shape[0]
    info = jnp.transpose(info_ref[...])
    results = jnp.concatenate([ref[...].astype(F32) for ref in result_refs], axis=0).astype(BF16)
    slots = lax.broadcasted_iota(jnp.int32, (rows, results.shape[0]), 1)
    picks = [
        jnp.where(slots == info[:, k : k + 1].astype(jnp.int32), 1.0, 0.0) for k in range(2)
    ]
    both = jnp.dot(
        jnp.concatenate(picks, axis=0).astype(BF16), results, preferred_element_type=F32
    )
    new = x_ref[...].astype(F32) + info[:, 2:3] * both[:rows] + info[:, 3:4] * both[rows:]
    out_ref[...] = new.astype(BF16)


def combine(x, info, results):
    rows, width = x.shape
    slots = len(results) * results[0].shape[0]
    return pl.pallas_call(
        combine_kernel,
        out_shape=jax.ShapeDtypeStruct((rows, width), BF16),
        in_specs=[VMEM] * (2 + len(results)),
        out_specs=VMEM,
        cost_estimate=pl.CostEstimate(
            flops=4 * rows * slots * width,
            bytes_accessed=2 * width * (2 * rows + slots),
            transcendentals=0,
        ),
        name="combine",
    )(x, info, *results)


def shards(carried, norm_gain, w_up, w_down, routes, gate_weights):
    experts = lax.axis_size("expert") // 4
    x = carried[0]
    tok_rows = x.shape[0]
    capacity = min(tok_rows, 4 * ((5 * tok_rows + 8 * experts - 1) // (8 * experts)))
    up, down = w_up[0].T, w_down[0]
    up_far, down_far = exchanged(up, 2), exchanged(down, 2)
    info, *rows = dispatch(x, norm_gain, routes[0, 0].T, gate_weights[0, 0].T, experts, capacity)
    rows = [rows[0]] + [exchanged(rows[d], 4 * d) for d in range(1, experts)]
    up_near, down_near = exchanged(up, 1), exchanged(down, 1)
    x_next, info_next = advanced(x, 0), advanced(info, 0)
    ups = (up, up_near, up_far, exchanged(up_far, 1))
    downs = (down, down_near, down_far, exchanged(down_far, 1))
    first = experts - experts // 4
    results = [
        advanced(result, 4 * d) for d, result in enumerate(ffn(rows[:first], ups, downs))
    ]
    results += [
        advanced(result, 4 * (first + d))
        for d, result in enumerate(ffn(rows[first:], ups, downs))
    ]
    return combine(x_next, info_next, results)[None]


def solution(mesh):
    in_specs = (
        P("section", "expert", None),
        P("section", None),
        P("section", None, "expert"),
        P("section", "expert", None),
        P(None, "section", "expert", None),
        P(None, "section", "expert", None),
    )
    out_specs = P("section", "expert", None)
    return jax.shard_map(shards, mesh=mesh, in_specs=in_specs, out_specs=out_specs, check_vma=False)
```

```python
import functools

import jax
import jax.numpy as jnp
from jax import lax
from jax.experimental import pallas as pl
from jax.experimental.pallas import tpu as pltpu
from jax.sharding import PartitionSpec as P


VMEM = pl.BlockSpec(memory_space=pltpu.VMEM)
ANY = pl.BlockSpec(memory_space=pl.ANY)
VMEM_LIMIT = 32 * 2**20
BF16, F32 = jnp.bfloat16, jnp.float32


def exchanged(value, distance):
    count = lax.axis_size("expert")
    return lax.ppermute(value, "expert", [(i, i ^ distance) for i in range(count)])


def advanced(value, distance):
    sections, count = lax.axis_size("section"), lax.axis_size("expert")
    pairs = [
        (s * count + i, (s + 1) % sections * count + (i ^ distance))
        for s in range(sections)
        for i in range(count)
    ]
    return lax.ppermute(value, ("section", "expert"), pairs)


def dispatch_kernel(experts, capacity, x_ref, gain_ref, routes_ref, gates_ref, info_ref, *out_refs):
    rows = x_ref.shape[0]
    own = lax.axis_index("expert") // 4
    r0, r1 = routes_ref[0:1, :], routes_ref[1:2, :]
    padded = max(experts, 8)
    ids = lax.broadcasted_iota(jnp.int32, (padded, rows), 0)
    named = jnp.where((ids == r0) | (ids == r1), 1.0, 0.0)
    before = lax.broadcasted_iota(jnp.int32, (rows, rows), 0) < lax.broadcasted_iota(
        jnp.int32, (rows, rows), 1
    )
    place = jnp.dot(
        named.astype(BF16), jnp.where(before, 1.0, 0.0).astype(BF16), preferred_element_type=F32
    )
    p0 = jnp.sum(jnp.where(ids == r0, place, 0.0), axis=0, keepdims=True)
    p1 = jnp.sum(jnp.where(ids == r1, place, 0.0), axis=0, keepdims=True)
    t0 = (r0 ^ own) * capacity + p0.astype(jnp.int32)
    t1 = (r1 ^ own) * capacity + p1.astype(jnp.int32)
    info_ref[0:1, :] = t0.astype(F32)
    info_ref[1:2, :] = t1.astype(F32)
    info_ref[2:4, :] = gates_ref[...]
    info_ref[4:8, :] = jnp.zeros((4, rows), F32)
    slots = lax.broadcasted_iota(jnp.int32, (experts * capacity, rows), 0)
    chosen = jnp.where((slots == t0) | (slots == t1), 1.0, 0.0).astype(BF16)
    values = x_ref[...].astype(F32)
    scale = lax.rsqrt(jnp.mean(values * values, axis=-1, keepdims=True) + 1e-05)
    normed = (values * scale * gain_ref[...]).astype(BF16)
    sent = jnp.dot(chosen, normed, preferred_element_type=F32)
    for d, out_ref in enumerate(out_refs):
        out_ref[...] = sent[d * capacity : (d + 1) * capacity].astype(BF16)


def dispatch(x, gain, routes, gates, experts, capacity):
    rows, width = x.shape
    return pl.pallas_call(
        functools.partial(dispatch_kernel, experts, capacity),
        out_shape=[jax.ShapeDtypeStruct((8, rows), F32)]
        + [jax.ShapeDtypeStruct((capacity, width), BF16)] * experts,
        in_specs=[VMEM] * 4,
        out_specs=[VMEM] * (experts + 1),
        cost_estimate=pl.CostEstimate(
            flops=2 * experts * capacity * rows * width,
            bytes_accessed=2 * width * (rows + experts * capacity),
            transcendentals=0,
        ),
        compiler_params=pltpu.CompilerParams(vmem_limit_bytes=VMEM_LIMIT),
        name="dispatch",
    )(x, gain, routes, gates)


def ffn_kernel(groups, *refs):
    row_refs, refs = refs[:groups], refs[groups:]
    up_refs, down_refs, refs = refs[:4], refs[4:8], refs[8:]
    out_refs, (up, down, sems) = refs[:groups], refs[groups:]
    quarter = up_refs[0].shape[0]
    copies = [
        pltpu.make_async_copy(src, dst.at[pl.ds(i * quarter, quarter)], sems.at[k, i])
        for k, (sources, dst) in enumerate(((up_refs, up), (down_refs, down)))
        for i, src in enumerate(sources)
    ]
    for copy in copies:
        copy.start()
    rows = jnp.concatenate([ref[...].astype(F32) for ref in row_refs], axis=0).astype(BF16)
    for copy in copies[:4]:
        copy.wait()
    hidden = lax.dot_general(
        rows, up[...], (((1,), (1,)), ((), ())), preferred_element_type=F32
    )
    hidden = jax.nn.gelu(hidden).astype(BF16)
    for copy in copies[4:]:
        copy.wait()
    out = jnp.dot(hidden, down[...], preferred_element_type=F32)
    capacity = out_refs[0].shape[0]
    for d, out_ref in enumerate(out_refs):
        out_ref[...] = out[d * capacity : (d + 1) * capacity].astype(BF16)


def ffn(rows, ups, downs):
    groups, (capacity, width) = len(rows), rows[0].shape
    quarter = ups[0].shape[0]
    return pl.pallas_call(
        functools.partial(ffn_kernel, groups),
        out_shape=[jax.ShapeDtypeStruct((capacity, width), BF16)] * groups,
        in_specs=[VMEM] * groups + [ANY] * 8,
        out_specs=[VMEM] * groups,
        scratch_shapes=[
            pltpu.VMEM((4 * quarter, width), BF16),
            pltpu.VMEM((4 * quarter, width), BF16),
            pltpu.SemaphoreType.DMA((2, 4)),
        ],
        cost_estimate=pl.CostEstimate(
            flops=16 * groups * capacity * quarter * width,
            bytes_accessed=4 * width * (groups * capacity + 4 * quarter),
            transcendentals=4 * groups * capacity * quarter,
        ),
        compiler_params=pltpu.CompilerParams(vmem_limit_bytes=VMEM_LIMIT),
        name="ffn",
    )(*rows, *ups, *downs)


def combine_kernel(x_ref, info_ref, *refs):
    result_refs, out_ref = refs[:-1], refs[-1]
    rows = x_ref.shape[0]
    info = jnp.transpose(info_ref[...])
    results = jnp.concatenate([ref[...].astype(F32) for ref in result_refs], axis=0).astype(BF16)
    slots = lax.broadcasted_iota(jnp.int32, (rows, results.shape[0]), 1)
    picks = [
        jnp.where(slots == info[:, k : k + 1].astype(jnp.int32), 1.0, 0.0) for k in range(2)
    ]
    both = jnp.dot(
        jnp.concatenate(picks, axis=0).astype(BF16), results, preferred_element_type=F32
    )
    new = x_ref[...].astype(F32) + info[:, 2:3] * both[:rows] + info[:, 3:4] * both[rows:]
    out_ref[...] = new.astype(BF16)


def combine(x, info, results):
    rows, width = x.shape
    slots = len(results) * results[0].shape[0]
    return pl.pallas_call(
        combine_kernel,
        out_shape=jax.ShapeDtypeStruct((rows, width), BF16),
        in_specs=[VMEM] * (2 + len(results)),
        out_specs=VMEM,
        cost_estimate=pl.CostEstimate(
            flops=4 * rows * slots * width,
            bytes_accessed=2 * width * (2 * rows + slots),
            transcendentals=0,
        ),
        compiler_params=pltpu.CompilerParams(vmem_limit_bytes=VMEM_LIMIT),
        name="combine",
    )(x, info, *results)


def step(carried, norm_gain, w_up, w_down, routes, gate_weights):
    experts = lax.axis_size("expert") // 4
    x = carried[0]
    tok_rows = x.shape[0]
    capacity = min(tok_rows, 4 * ((5 * tok_rows + 8 * experts - 1) // (8 * experts)))
    up, down = w_up[0].T, w_down[0]
    up_far, down_far = exchanged(up, 2), exchanged(down, 2)
    info, *rows = dispatch(x, norm_gain, routes[0, 0].T, gate_weights[0, 0].T, experts, capacity)
    rows = [rows[0]] + [exchanged(rows[d], 4 * d) for d in range(1, experts)]
    up_near, down_near = exchanged(up, 1), exchanged(down, 1)
    x_next, info_next = advanced(x, 0), advanced(info, 0)
    ups = (up, up_near, up_far, exchanged(up_far, 1))
    downs = (down, down_near, down_far, exchanged(down_far, 1))
    first = experts - experts // 4
    early = ffn(rows[:first], ups, downs)
    results = [advanced(early[d], 4 * d) for d in range(first)]
    late = ffn(rows[first:], ups, downs)
    results += [advanced(late[d - first], 4 * d) for d in range(first, experts)]
    return combine(x_next, info_next, results)[None]


def solution(mesh):
    in_specs = (
        P("section", "expert", None),
        P("section", None),
        P("section", None, "expert"),
        P("section", "expert", None),
        P(None, "section", "expert", None),
        P(None, "section", "expert", None),
    )
    out_specs = P("section", "expert", None)
    return jax.shard_map(step, mesh=mesh, in_specs=in_specs, out_specs=out_specs, check_vma=False)
```

```python
import functools

import jax
import jax.numpy as jnp
from jax import lax
from jax.experimental import pallas as pl
from jax.experimental.pallas import tpu as pltpu
from jax.sharding import PartitionSpec as P


VMEM = pl.BlockSpec(memory_space=pltpu.VMEM)
VMEM_LIMIT = 32 * 2**20
BF16, F32 = jnp.bfloat16, jnp.float32


def exchanged(value, distance):
    count = lax.axis_size("expert")
    return lax.ppermute(value, "expert", [(i, i ^ distance) for i in range(count)])


def advanced(value, distance):
    sections, count = lax.axis_size("section"), lax.axis_size("expert")
    pairs = [
        (s * count + i, (s + 1) % sections * count + (i ^ distance))
        for s in range(sections)
        for i in range(count)
    ]
    return lax.ppermute(value, ("section", "expert"), pairs)


def slots_of(routes, blocks, capacity):
    rows = routes.shape[1]
    own = lax.axis_index("expert") // 4
    named = [routes[k : k + 1, :] for k in range(2)]
    ids = lax.broadcasted_iota(jnp.int32, (max(blocks, 8), rows), 0)
    both = jnp.where((ids == named[0]) | (ids == named[1]), 1.0, 0.0).astype(BF16)
    before = lax.broadcasted_iota(jnp.int32, (rows, rows), 0) < lax.broadcasted_iota(
        jnp.int32, (rows, rows), 1
    )
    place = jnp.dot(both, jnp.where(before, 1.0, 0.0).astype(BF16), preferred_element_type=F32)
    return [
        (r ^ own) * capacity
        + jnp.sum(jnp.where(ids == r, place, 0.0), axis=0, keepdims=True).astype(jnp.int32)
        for r in named
    ]


def sort_kernel(capacity, x_ref, routes_ref, *out_refs):
    blocks = len(out_refs)
    s0, s1 = slots_of(routes_ref[...], blocks, capacity)
    ids = lax.broadcasted_iota(jnp.int32, (blocks * capacity, x_ref.shape[0]), 0)
    chosen = jnp.where((ids == s0) | (ids == s1), 1.0, 0.0).astype(BF16)
    sent = jnp.dot(chosen, x_ref[...], preferred_element_type=F32)
    for d, out_ref in enumerate(out_refs):
        out_ref[...] = sent[d * capacity : (d + 1) * capacity].astype(BF16)


def sort(x, routes, blocks, capacity):
    rows, width = x.shape
    return pl.pallas_call(
        functools.partial(sort_kernel, capacity),
        out_shape=[jax.ShapeDtypeStruct((capacity, width), BF16)] * blocks,
        in_specs=[VMEM] * 2,
        out_specs=[VMEM] * blocks,
        cost_estimate=pl.CostEstimate(
            flops=2 * blocks * capacity * rows * width,
            bytes_accessed=2 * width * (rows + blocks * capacity),
            transcendentals=0,
        ),
        compiler_params=pltpu.CompilerParams(vmem_limit_bytes=VMEM_LIMIT),
        name="sort",
    )(x, routes)


def joined(sources, target, sems):
    size = sources[0].shape[0]
    copies = [
        pltpu.make_async_copy(src, target.at[pl.ds(i * size, size)], sems.at[i])
        for i, src in enumerate(sources)
    ]
    for copy in copies:
        copy.start()

    def read():
        for copy in copies:
            copy.wait()
        return target[...]

    return read


def hidden_of(row_refs, gain, up):
    values = jnp.concatenate([ref[...].astype(F32) for ref in row_refs], axis=0)
    scale = lax.rsqrt(jnp.mean(values * values, axis=-1, keepdims=True) + 1e-05)
    rows = (values * scale * gain).astype(BF16)
    hidden = lax.dot_general(rows, up(), (((1,), (1,)), ((), ())), preferred_element_type=F32)
    return jax.nn.gelu(hidden)


def outputs_of(hidden, down, out_refs):
    out = jnp.dot(hidden, down, preferred_element_type=F32)
    capacity = out_refs[0].shape[0]
    for d, out_ref in enumerate(out_refs):
        out_ref[...] = out[d * capacity : (d + 1) * capacity].astype(BF16)


def up_kernel(groups, *refs):
    gain_ref, up_refs = refs[groups], refs[groups + 1 : groups + 5]
    own_ref, hidden_ref, up_ref, sems = refs[groups + 5 :]
    hidden = hidden_of(refs[:groups], gain_ref[...], joined(up_refs, up_ref, sems))
    capacity = own_ref.shape[0]
    own_ref[...] = hidden[:capacity].astype(BF16)
    hidden_ref[...] = hidden[capacity:].astype(BF16)


def down_kernel(groups, hidden_ref, *refs):
    down_refs, (*out_refs, down_ref, sems) = refs[:4], refs[4:]
    outputs_of(hidden_ref[...], joined(down_refs, down_ref, sems)(), out_refs)


def home_kernel(groups, hidden_ref, *refs):
    *down_refs, out_ref = refs
    size = down_refs[0].shape[0]
    hidden = hidden_ref[...]
    out_ref[...] = sum(
        jnp.dot(hidden[:, i * size : (i + 1) * size], ref[...], preferred_element_type=F32)
        for i, ref in enumerate(down_refs)
    ).astype(BF16)


def ffn_kernel(groups, *refs):
    gain_ref, up_ref, down_ref = refs[groups : groups + 3]
    hidden = hidden_of(refs[:groups], gain_ref[...], lambda: up_ref[...])
    outputs_of(hidden.astype(BF16), down_ref[...], refs[groups + 3 :])


def expert_call(kernel, groups, inputs, outs, shape, products):
    (capacity, width), units = shape
    rows = groups * capacity
    return pl.pallas_call(
        functools.partial(kernel, groups),
        out_shape=[jax.ShapeDtypeStruct(shape, BF16) for shape in outs],
        in_specs=[VMEM] * len(inputs),
        out_specs=[VMEM] * len(outs),
        scratch_shapes=[pltpu.SemaphoreType.DMA((4,))] if kernel in (up_kernel, down_kernel) else [],
        cost_estimate=pl.CostEstimate(
            flops=2 * products * rows * units * width,
            bytes_accessed=2 * products * width * (rows + units),
            transcendentals=rows * units,
        ),
        compiler_params=pltpu.CompilerParams(vmem_limit_bytes=VMEM_LIMIT),
    )(*inputs)


def slot_weights(info, first, count, dtype):
    slots = first + lax.broadcasted_iota(jnp.int32, (info.shape[0], count), 1)
    return sum(
        jnp.where(slots == info[:, k : k + 1].astype(jnp.int32), info[:, k + 2 : k + 3], 0.0)
        for k in range(2)
    ).astype(dtype)


def parts_of(weights):
    high = weights.astype(BF16)
    return high, (weights - high.astype(F32)).astype(BF16)


def taken(high, low, results):
    return jnp.dot(high, results, preferred_element_type=F32) + jnp.dot(
        low, results, preferred_element_type=F32
    )


def mix_kernel(blocks, x_ref, routes_ref, gates_ref, *refs):
    result_refs, (sum_ref, high_ref, low_ref) = refs[:-3], refs[-3:]
    capacity = result_refs[0].shape[0]
    slots = [s.astype(F32) for s in slots_of(routes_ref[...], blocks, capacity)]
    rows = slots[0].shape[1]
    info = jnp.concatenate(slots + [gates_ref[...], jnp.zeros((4, rows), F32)], axis=0)
    info = jnp.transpose(info)
    results = jnp.concatenate([ref[...].astype(F32) for ref in result_refs], axis=0).astype(BF16)
    count = results.shape[0]
    high, low = parts_of(slot_weights(info, 0, count, F32))
    sum_ref[...] = x_ref[...].astype(F32) + taken(high, low, results)
    high_ref[...], low_ref[...] = parts_of(
        slot_weights(info, count, blocks * capacity - count, F32)
    )


def last_kernel(sum_ref, high_ref, low_ref, *refs):
    results = jnp.concatenate([ref[...].astype(F32) for ref in refs[:-1]], axis=0).astype(BF16)
    refs[-1][...] = (sum_ref[...] + taken(high_ref[...], low_ref[...], results)).astype(BF16)


def combine_call(kernel, inputs, out_shape, slots):
    rows, width = inputs[0].shape
    return pl.pallas_call(
        kernel,
        out_shape=out_shape,
        in_specs=[VMEM] * len(inputs),
        out_specs=[VMEM] * len(out_shape),
        cost_estimate=pl.CostEstimate(
            flops=4 * rows * slots * width,
            bytes_accessed=2 * width * (3 * rows + slots),
            transcendentals=0,
        ),
        compiler_params=pltpu.CompilerParams(vmem_limit_bytes=VMEM_LIMIT),
    )(*inputs)


def step(carried, norm_gain, w_up, w_down, routes, gate_weights):
    experts = lax.axis_size("expert") // 4
    first = experts - experts // 4
    x, routes_now = carried[0], routes[0, 0].T
    tok_rows, width = x.shape
    capacity = min(tok_rows, 4 * ((5 * tok_rows + 8 * experts - 1) // (8 * experts)))
    block = (capacity, width)
    up, down = w_up[0].T, w_down[0]
    units = (4 * up.shape[0], width)
    shape = (block, units[0])

    rows = sort(x, routes_now, experts, capacity)
    rows = [rows[0]] + [exchanged(rows[d], 4 * d) for d in range(1, experts)]
    up_far, down_far = exchanged(up, 2), exchanged(down, 2)
    up_near, down_near = exchanged(up, 1), exchanged(down, 1)
    x_next = advanced(x, 0)
    routes_next = advanced(routes_now, 0)
    gates_next = advanced(gate_weights[0, 0].T, 0)
    ups = [up, up_near, up_far, exchanged(up_far, 1)]
    downs = [down, down_near, down_far, exchanged(down_far, 1)]
    hidden_own, hidden, up_all = expert_call(
        up_kernel,
        first,
        [*rows[:first], norm_gain, *ups],
        [(capacity, units[0]), ((first - 1) * capacity, units[0]), units],
        shape,
        1,
    )
    *early, down_all = expert_call(
        down_kernel, first - 1, [hidden, *downs], [block] * (first - 1) + [units], shape, 1
    )
    hidden_next = advanced(hidden_own, 0)
    down_next = advanced(down, 0)
    down_next_far = exchanged(down_next, 2)
    downs_next = [down_next, exchanged(down_next, 1)]
    downs_next += [down_next_far, exchanged(down_next_far, 1)]
    (home,) = expert_call(home_kernel, 1, [hidden_next, *downs_next], [block], shape, 1)
    late = expert_call(
        ffn_kernel,
        experts - first,
        [*rows[first:], norm_gain, up_all, down_all],
        [block] * (experts - first),
        shape,
        2,
    )
    results = [home] + [advanced(rows, 4 * (d + 1)) for d, rows in enumerate([*early, *late])]
    count = (experts - first) * capacity
    sums = combine_call(
        functools.partial(mix_kernel, experts),
        [x_next, routes_next, gates_next] + results[:first],
        [jax.ShapeDtypeStruct(x.shape, F32)]
        + [jax.ShapeDtypeStruct((tok_rows, count), BF16)] * 2,
        first * capacity,
    )
    (out,) = combine_call(
        last_kernel, [*sums, *results[first:]], [jax.ShapeDtypeStruct(x.shape, BF16)], count
    )
    return out[None]


def solution(mesh):
    in_specs = (
        P("section", "expert", None),
        P("section", None),
        P("section", None, "expert"),
        P("section", "expert", None),
        P(None, "section", "expert", None),
        P(None, "section", "expert", None),
    )
    out_specs = P("section", "expert", None)
    return jax.shard_map(step, mesh=mesh, in_specs=in_specs, out_specs=out_specs, check_vma=False)
```

```python
import functools

import jax
import jax.numpy as jnp
from jax import lax
from jax.experimental import pallas as pl
from jax.experimental.pallas import tpu as pltpu
from jax.sharding import PartitionSpec as P


VMEM = pl.BlockSpec(memory_space=pltpu.VMEM)
VMEM_LIMIT = 32 * 2**20
BF16, F32 = jnp.bfloat16, jnp.float32


def exchanged(value, distance):
    count = lax.axis_size("expert")
    return lax.ppermute(value, "expert", [(i, i ^ distance) for i in range(count)])


def advanced(value, distance):
    sections, count = lax.axis_size("section"), lax.axis_size("expert")
    pairs = [
        (s * count + i, (s + 1) % sections * count + (i ^ distance))
        for s in range(sections)
        for i in range(count)
    ]
    return lax.ppermute(value, ("section", "expert"), pairs)


def place_of(distance, half):
    return distance + (distance >= half) * (3 * half - 1 - 2 * distance)


def sort_kernel(blocks, capacity, with_info, x_ref, gain_ref, routes_ref, *refs):
    out_refs = refs[-blocks:]
    rows = x_ref.shape[0]
    own = lax.axis_index("expert") // 4
    r0, r1 = routes_ref[0:1, :], routes_ref[1:2, :]
    ids = lax.broadcasted_iota(jnp.int32, (max(2 * blocks, 8), rows), 0)
    named = jnp.where((ids == r0) | (ids == r1), 1.0, 0.0)
    before = lax.broadcasted_iota(jnp.int32, (rows, rows), 0) < lax.broadcasted_iota(
        jnp.int32, (rows, rows), 1
    )
    place = jnp.dot(
        named.astype(BF16), jnp.where(before, 1.0, 0.0).astype(BF16), preferred_element_type=F32
    )
    p0 = jnp.sum(jnp.where(ids == r0, place, 0.0), axis=0, keepdims=True)
    p1 = jnp.sum(jnp.where(ids == r1, place, 0.0), axis=0, keepdims=True)
    t0 = place_of(r0 ^ own, blocks) * capacity + p0.astype(jnp.int32)
    t1 = place_of(r1 ^ own, blocks) * capacity + p1.astype(jnp.int32)
    if with_info:
        gates_ref, info_ref = refs[:2]
        info_ref[0:1, :] = t0.astype(F32)
        info_ref[1:2, :] = t1.astype(F32)
        info_ref[2:4, :] = gates_ref[...]
        info_ref[4:8, :] = jnp.zeros((4, rows), F32)
    slots = lax.broadcasted_iota(jnp.int32, (blocks * capacity, rows), 0)
    chosen = jnp.where((slots == t0) | (slots == t1), 1.0, 0.0).astype(BF16)
    values = x_ref[...].astype(F32)
    scale = lax.rsqrt(jnp.mean(values * values, axis=-1, keepdims=True) + 1e-05)
    normed = (values * scale * gain_ref[...]).astype(BF16)
    sent = jnp.dot(chosen, normed, preferred_element_type=F32)
    for d, out_ref in enumerate(out_refs):
        out_ref[...] = sent[d * capacity : (d + 1) * capacity].astype(BF16)


def sort(x, gain, routes, gates, blocks, capacity):
    rows, width = x.shape
    with_info = gates is not None
    out_shape = [jax.ShapeDtypeStruct((8, rows), F32)] if with_info else []
    out_shape += [jax.ShapeDtypeStruct((capacity, width), BF16)] * blocks
    inputs = (x, gain, routes) + ((gates,) if with_info else ())
    return pl.pallas_call(
        functools.partial(sort_kernel, blocks, capacity, with_info),
        out_shape=out_shape,
        in_specs=[VMEM] * len(inputs),
        out_specs=[VMEM] * len(out_shape),
        cost_estimate=pl.CostEstimate(
            flops=2 * blocks * capacity * rows * width,
            bytes_accessed=2 * width * (rows + blocks * capacity),
            transcendentals=0,
        ),
        compiler_params=pltpu.CompilerParams(vmem_limit_bytes=VMEM_LIMIT),
        name="sort",
    )(*inputs)


def joined(sources, target, sems):
    size = sources[0].shape[0]
    copies = [
        pltpu.make_async_copy(src, target.at[pl.ds(i * size, size)], sems.at[i])
        for i, src in enumerate(sources)
    ]
    for copy in copies:
        copy.start()

    def read():
        for copy in copies:
            copy.wait()
        return target[...]

    return read


def hidden_of(row_refs, up):
    rows = jnp.concatenate([ref[...].astype(F32) for ref in row_refs], axis=0).astype(BF16)
    hidden = lax.dot_general(rows, up, (((1,), (1,)), ((), ())), preferred_element_type=F32)
    return jax.nn.gelu(hidden)


def outputs_of(hidden, down, out_refs):
    out = jnp.dot(hidden, down, preferred_element_type=F32)
    capacity = out_refs[0].shape[0]
    for d, out_ref in enumerate(out_refs):
        out_ref[...] = out[d * capacity : (d + 1) * capacity].astype(BF16)


def up_kernel(groups, *refs):
    own_ref, near_ref, up_ref, sems = refs[groups + 4 :]
    read = joined(refs[groups : groups + 4], up_ref, sems)
    hidden = hidden_of(refs[:groups], read())
    capacity = own_ref.shape[0]
    own_ref[...] = hidden[:capacity].astype(BF16)
    near_ref[...] = hidden[capacity:].astype(BF16)


def far_kernel(groups, *refs):
    up_ref, down_refs = refs[groups], refs[groups + 1 : groups + 5]
    *out_refs, down_ref, sems = refs[groups + 5 :]
    read = joined(down_refs, down_ref, sems)
    hidden = hidden_of(refs[:groups], up_ref[...])
    outputs_of(hidden.astype(BF16), read(), out_refs)


def down_kernel(groups, hidden_ref, down_ref, *out_refs):
    outputs_of(hidden_ref[...], down_ref[...], out_refs)


def ffn_kernel(groups, *refs):
    up_ref, down_ref = refs[groups : groups + 2]
    hidden = hidden_of(refs[:groups], up_ref[...]).astype(BF16)
    outputs_of(hidden, down_ref[...], refs[groups + 2 :])


def home_kernel(groups, hidden_ref, *refs):
    *down_refs, out_ref = refs
    size = down_refs[0].shape[0]
    hidden = hidden_ref[...]
    out_ref[...] = sum(
        jnp.dot(hidden[:, i * size : (i + 1) * size], ref[...], preferred_element_type=F32)
        for i, ref in enumerate(down_refs)
    ).astype(BF16)


def expert_call(kernel, groups, inputs, outs, shape, products):
    (capacity, width), units = shape
    rows = groups * capacity
    return pl.pallas_call(
        functools.partial(kernel, groups),
        out_shape=[jax.ShapeDtypeStruct(shape, BF16) for shape in outs],
        in_specs=[VMEM] * len(inputs),
        out_specs=[VMEM] * len(outs),
        scratch_shapes=[pltpu.SemaphoreType.DMA((4,))] if kernel in (up_kernel, far_kernel) else [],
        cost_estimate=pl.CostEstimate(
            flops=2 * products * rows * units * width,
            bytes_accessed=2 * products * width * (rows + units),
            transcendentals=rows * units,
        ),
        compiler_params=pltpu.CompilerParams(vmem_limit_bytes=VMEM_LIMIT),
    )(*inputs)


def slot_weights(info, first, count, dtype):
    slots = first + lax.broadcasted_iota(jnp.int32, (info.shape[0], count), 1)
    return sum(
        jnp.where(slots == info[:, k : k + 1].astype(jnp.int32), info[:, k + 2 : k + 3], 0.0)
        for k in range(2)
    ).astype(dtype)


def parts_of(weights):
    high = weights.astype(BF16)
    return high, (weights - high.astype(F32)).astype(BF16)


def taken(high, low, results):
    return jnp.dot(high, results, preferred_element_type=F32) + jnp.dot(
        low, results, preferred_element_type=F32
    )


def mix_kernel(late, x_ref, info_ref, *refs):
    result_refs, (sum_ref, high_ref, low_ref) = refs[:-3], refs[-3:]
    info = jnp.transpose(info_ref[...])
    results = jnp.concatenate([ref[...].astype(F32) for ref in result_refs], axis=0).astype(BF16)
    count = results.shape[0]
    high, low = parts_of(slot_weights(info, 0, count, F32))
    sum_ref[...] = x_ref[...].astype(F32) + taken(high, low, results)
    high_ref[...], low_ref[...] = parts_of(slot_weights(info, count, late, F32))


def last_kernel(sum_ref, high_ref, low_ref, *refs):
    results = jnp.concatenate([ref[...].astype(F32) for ref in refs[:-1]], axis=0).astype(BF16)
    refs[-1][...] = (sum_ref[...] + taken(high_ref[...], low_ref[...], results)).astype(BF16)


def combine_call(kernel, inputs, out_shape, slots):
    rows, width = inputs[0].shape
    return pl.pallas_call(
        kernel,
        out_shape=out_shape,
        in_specs=[VMEM] * len(inputs),
        out_specs=[VMEM] * len(out_shape),
        cost_estimate=pl.CostEstimate(
            flops=4 * rows * slots * width,
            bytes_accessed=2 * width * (3 * rows + slots),
            transcendentals=0,
        ),
        compiler_params=pltpu.CompilerParams(vmem_limit_bytes=VMEM_LIMIT),
    )(*inputs)


def step(carried, norm_gain, w_up, w_down, routes, gate_weights):
    half = lax.axis_size("expert") // 8
    x, routes_now = carried[0], routes[0, 0].T
    tok_rows, width = x.shape
    capacity = min(tok_rows, 4 * ((5 * tok_rows + 16 * half - 1) // (16 * half)))
    block = (capacity, width)
    up, down = w_up[0].T, w_down[0]
    units = (4 * up.shape[0], width)
    shape = (block, units[0])

    far_x = exchanged(x, 4 * (2 * half - 1))
    far_routes = exchanged(routes_now, 4 * (2 * half - 1))
    up_far, down_far = exchanged(up, 2), exchanged(down, 2)
    info, *own = sort(x, norm_gain, routes_now, gate_weights[0, 0].T, half, capacity)
    near = own[:1] + [exchanged(own[d], 4 * d) for d in range(1, half)]
    up_near, down_near = exchanged(up, 1), exchanged(down, 1)
    x_next, info_next = advanced(x, 0), advanced(info, 0)
    down_next = advanced(down, 0)
    down_next_far = exchanged(down_next, 2)
    downs_next = [down_next, exchanged(down_next, 1)]
    downs_next += [down_next_far, exchanged(down_next_far, 1)]
    ups = [up, up_near, up_far, exchanged(up_far, 1)]
    downs = [down, down_near, down_far, exchanged(down_far, 1)]
    hidden_own, hidden, up_all = expert_call(
        up_kernel,
        half,
        near + ups,
        [(capacity, units[0]), ((half - 1) * capacity, units[0]), units],
        shape,
        1,
    )
    hidden_next = advanced(hidden_own, 0)
    far, *relayed = sort(far_x, norm_gain, far_routes, None, half, capacity)
    relayed = [exchanged(rows, 4 * (d + 1)) for d, rows in enumerate(relayed)]
    far, down_all = expert_call(far_kernel, 1, [far, up_all] + downs, [block, units], shape, 2)
    near = expert_call(down_kernel, half - 1, [hidden, down_all], [block] * (half - 1), shape, 1)
    late = expert_call(
        ffn_kernel, half - 1, relayed + [up_all, down_all], [block] * (half - 1), shape, 2
    )
    results = list(expert_call(home_kernel, 1, [hidden_next] + downs_next, [block], shape, 1))
    results += [
        advanced(rows, 4 * place_of(d, half))
        for d, rows in enumerate([*near, far, *late], 1)
    ]
    count = (half - 1) * capacity
    sums = combine_call(
        functools.partial(mix_kernel, count),
        [x_next, info_next] + results[: half + 1],
        [jax.ShapeDtypeStruct(x.shape, F32)]
        + [jax.ShapeDtypeStruct((tok_rows, count), BF16)] * 2,
        (half + 1) * capacity,
    )
    (out,) = combine_call(
        last_kernel, [*sums, *results[half + 1 :]], [jax.ShapeDtypeStruct(x.shape, BF16)], count
    )
    return out[None]


def solution(mesh):
    in_specs = (
        P("section", "expert", None),
        P("section", None),
        P("section", None, "expert"),
        P("section", "expert", None),
        P(None, "section", "expert", None),
        P(None, "section", "expert", None),
    )
    out_specs = P("section", "expert", None)
    return jax.shard_map(step, mesh=mesh, in_specs=in_specs, out_specs=out_specs, check_vma=False)
```

```python
import functools

import jax
import jax.numpy as jnp
from jax import lax
from jax.experimental import pallas as pl
from jax.experimental.pallas import tpu as pltpu
from jax.sharding import PartitionSpec as P


VMEM = pl.BlockSpec(memory_space=pltpu.VMEM)
VMEM_LIMIT = 32 * 2**20
BF16, F32 = jnp.bfloat16, jnp.float32


def exchanged(value, distance):
    count = lax.axis_size("expert")
    return lax.ppermute(value, "expert", [(i, i ^ distance) for i in range(count)])


def advanced(value, distance):
    sections, count = lax.axis_size("section"), lax.axis_size("expert")
    pairs = [
        (s * count + i, (s + 1) % sections * count + (i ^ distance))
        for s in range(sections)
        for i in range(count)
    ]
    return lax.ppermute(value, ("section", "expert"), pairs)


def place_of(distance, half):
    return distance + (distance >= half) * (3 * half - 1 - 2 * distance)


def sort_kernel(blocks, capacity, with_info, x_ref, gain_ref, routes_ref, *refs):
    out_refs = refs[-blocks:]
    rows = x_ref.shape[0]
    own = lax.axis_index("expert") // 4
    r0, r1 = routes_ref[0:1, :], routes_ref[1:2, :]
    ids = lax.broadcasted_iota(jnp.int32, (max(2 * blocks, 8), rows), 0)
    named = jnp.where((ids == r0) | (ids == r1), 1.0, 0.0)
    before = lax.broadcasted_iota(jnp.int32, (rows, rows), 0) < lax.broadcasted_iota(
        jnp.int32, (rows, rows), 1
    )
    place = jnp.dot(
        named.astype(BF16), jnp.where(before, 1.0, 0.0).astype(BF16), preferred_element_type=F32
    )
    p0 = jnp.sum(jnp.where(ids == r0, place, 0.0), axis=0, keepdims=True)
    p1 = jnp.sum(jnp.where(ids == r1, place, 0.0), axis=0, keepdims=True)
    t0 = place_of(r0 ^ own, blocks) * capacity + p0.astype(jnp.int32)
    t1 = place_of(r1 ^ own, blocks) * capacity + p1.astype(jnp.int32)
    if with_info:
        gates_ref, info_ref = refs[:2]
        info_ref[0:1, :] = t0.astype(F32)
        info_ref[1:2, :] = t1.astype(F32)
        info_ref[2:4, :] = gates_ref[...]
        info_ref[4:8, :] = jnp.zeros((4, rows), F32)
    slots = lax.broadcasted_iota(jnp.int32, (blocks * capacity, rows), 0)
    chosen = jnp.where((slots == t0) | (slots == t1), 1.0, 0.0).astype(BF16)
    values = x_ref[...].astype(F32)
    scale = lax.rsqrt(jnp.mean(values * values, axis=-1, keepdims=True) + 1e-05)
    normed = (values * scale * gain_ref[...]).astype(BF16)
    sent = jnp.dot(chosen, normed, preferred_element_type=F32)
    for d, out_ref in enumerate(out_refs):
        out_ref[...] = sent[d * capacity : (d + 1) * capacity].astype(BF16)


def sort(x, gain, routes, gates, blocks, capacity):
    rows, width = x.shape
    with_info = gates is not None
    out_shape = [jax.ShapeDtypeStruct((8, rows), F32)] if with_info else []
    out_shape += [jax.ShapeDtypeStruct((capacity, width), BF16)] * blocks
    inputs = (x, gain, routes) + ((gates,) if with_info else ())
    return pl.pallas_call(
        functools.partial(sort_kernel, blocks, capacity, with_info),
        out_shape=out_shape,
        in_specs=[VMEM] * len(inputs),
        out_specs=[VMEM] * len(out_shape),
        cost_estimate=pl.CostEstimate(
            flops=2 * blocks * capacity * rows * width,
            bytes_accessed=2 * width * (rows + blocks * capacity),
            transcendentals=0,
        ),
        compiler_params=pltpu.CompilerParams(vmem_limit_bytes=VMEM_LIMIT),
        name="sort",
    )(*inputs)


def joined(sources, target, sems):
    size = sources[0].shape[0]
    copies = [
        pltpu.make_async_copy(src, target.at[pl.ds(i * size, size)], sems.at[i])
        for i, src in enumerate(sources)
    ]
    for copy in copies:
        copy.start()

    def read():
        for copy in copies:
            copy.wait()
        return target[...]

    return read


def hidden_of(row_refs, up):
    rows = jnp.concatenate([ref[...].astype(F32) for ref in row_refs], axis=0).astype(BF16)
    hidden = lax.dot_general(rows, up, (((1,), (1,)), ((), ())), preferred_element_type=F32)
    return jax.nn.gelu(hidden)


def outputs_of(hidden, down, out_refs):
    out = jnp.dot(hidden, down, preferred_element_type=F32)
    capacity = out_refs[0].shape[0]
    for d, out_ref in enumerate(out_refs):
        out_ref[...] = out[d * capacity : (d + 1) * capacity].astype(BF16)


def up_kernel(groups, *refs):
    own_ref, near_ref, up_ref, sems = refs[groups + 4 :]
    read = joined(refs[groups : groups + 4], up_ref, sems)
    hidden = hidden_of(refs[:groups], read())
    capacity = own_ref.shape[0]
    own_ref[...] = hidden[:capacity].astype(BF16)
    near_ref[...] = hidden[capacity:].astype(BF16)


def rise_kernel(groups, *refs):
    refs[-1][...] = hidden_of(refs[:groups], refs[groups][...]).astype(BF16)


def fall_kernel(groups, hidden_ref, *refs):
    *out_refs, down_ref, sems = refs[4:]
    outputs_of(hidden_ref[...], joined(refs[:4], down_ref, sems)(), out_refs)


def down_kernel(groups, hidden_ref, down_ref, *out_refs):
    outputs_of(hidden_ref[...], down_ref[...], out_refs)


def ffn_kernel(groups, *refs):
    up_ref, down_ref = refs[groups : groups + 2]
    hidden = hidden_of(refs[:groups], up_ref[...]).astype(BF16)
    outputs_of(hidden, down_ref[...], refs[groups + 2 :])


def home_kernel(groups, hidden_ref, *refs):
    *down_refs, out_ref = refs
    size = down_refs[0].shape[0]
    hidden = hidden_ref[...]
    out_ref[...] = sum(
        jnp.dot(hidden[:, i * size : (i + 1) * size], ref[...], preferred_element_type=F32)
        for i, ref in enumerate(down_refs)
    ).astype(BF16)


def expert_call(kernel, groups, inputs, outs, shape, products):
    (capacity, width), units = shape
    rows = groups * capacity
    return pl.pallas_call(
        functools.partial(kernel, groups),
        out_shape=[jax.ShapeDtypeStruct(shape, BF16) for shape in outs],
        in_specs=[VMEM] * len(inputs),
        out_specs=[VMEM] * len(outs),
        scratch_shapes=[pltpu.SemaphoreType.DMA((4,))] if kernel in (up_kernel, fall_kernel) else [],
        cost_estimate=pl.CostEstimate(
            flops=2 * products * rows * units * width,
            bytes_accessed=2 * products * width * (rows + units),
            transcendentals=rows * units,
        ),
        compiler_params=pltpu.CompilerParams(vmem_limit_bytes=VMEM_LIMIT),
    )(*inputs)


def slot_weights(info, first, count, dtype):
    slots = first + lax.broadcasted_iota(jnp.int32, (info.shape[0], count), 1)
    return sum(
        jnp.where(slots == info[:, k : k + 1].astype(jnp.int32), info[:, k + 2 : k + 3], 0.0)
        for k in range(2)
    ).astype(dtype)


def parts_of(weights):
    high = weights.astype(BF16)
    return high, (weights - high.astype(F32)).astype(BF16)


def taken(high, low, results):
    return jnp.dot(high, results, preferred_element_type=F32) + jnp.dot(
        low, results, preferred_element_type=F32
    )


def mix_kernel(late, x_ref, info_ref, *refs):
    result_refs, (sum_ref, high_ref, low_ref) = refs[:-3], refs[-3:]
    info = jnp.transpose(info_ref[...])
    results = jnp.concatenate([ref[...].astype(F32) for ref in result_refs], axis=0).astype(BF16)
    count = results.shape[0]
    high, low = parts_of(slot_weights(info, 0, count, F32))
    sum_ref[...] = x_ref[...].astype(F32) + taken(high, low, results)
    high_ref[...], low_ref[...] = parts_of(slot_weights(info, count, late, F32))


def last_kernel(sum_ref, high_ref, low_ref, *refs):
    results = jnp.concatenate([ref[...].astype(F32) for ref in refs[:-1]], axis=0).astype(BF16)
    refs[-1][...] = (sum_ref[...] + taken(high_ref[...], low_ref[...], results)).astype(BF16)


def combine_call(kernel, inputs, out_shape, slots):
    rows, width = inputs[0].shape
    return pl.pallas_call(
        kernel,
        out_shape=out_shape,
        in_specs=[VMEM] * len(inputs),
        out_specs=[VMEM] * len(out_shape),
        cost_estimate=pl.CostEstimate(
            flops=4 * rows * slots * width,
            bytes_accessed=2 * width * (3 * rows + slots),
            transcendentals=0,
        ),
        compiler_params=pltpu.CompilerParams(vmem_limit_bytes=VMEM_LIMIT),
    )(*inputs)


def step(carried, norm_gain, w_up, w_down, routes, gate_weights):
    half = lax.axis_size("expert") // 8
    x, routes_now = carried[0], routes[0, 0].T
    tok_rows, width = x.shape
    capacity = min(tok_rows, 4 * ((5 * tok_rows + 16 * half - 1) // (16 * half)))
    block = (capacity, width)
    up, down = w_up[0].T, w_down[0]
    units = (4 * up.shape[0], width)
    shape = (block, units[0])

    far_x = exchanged(x, 4 * (2 * half - 1))
    far_routes = exchanged(routes_now, 4 * (2 * half - 1))
    up_far, down_far = exchanged(up, 2), exchanged(down, 2)
    info, *own = sort(x, norm_gain, routes_now, gate_weights[0, 0].T, half, capacity)
    near = own[:1] + [exchanged(own[d], 4 * d) for d in range(1, half)]
    up_near, down_near = exchanged(up, 1), exchanged(down, 1)
    x_next, info_next = advanced(x, 0), advanced(info, 0)
    down_next = advanced(down, 0)
    down_next_far = exchanged(down_next, 2)
    downs_next = [down_next, exchanged(down_next, 1)]
    downs_next += [down_next_far, exchanged(down_next_far, 1)]
    ups = [up, up_near, up_far, exchanged(up_far, 1)]
    downs = [down, down_near, down_far, exchanged(down_far, 1)]
    hidden_own, hidden, up_all = expert_call(
        up_kernel,
        half,
        near + ups,
        [(capacity, units[0]), ((half - 1) * capacity, units[0]), units],
        shape,
        1,
    )
    hidden_next = advanced(hidden_own, 0)
    far, *relayed = sort(far_x, norm_gain, far_routes, None, half, capacity)
    relayed = [exchanged(rows, 4 * (d + 1)) for d, rows in enumerate(relayed)]
    (rise,) = expert_call(rise_kernel, 1, [far, up_all], [(capacity, units[0])], shape, 1)
    far, down_all = expert_call(fall_kernel, 1, [rise, *downs], [block, units], shape, 1)
    near = expert_call(down_kernel, half - 1, [hidden, down_all], [block] * (half - 1), shape, 1)
    late = expert_call(
        ffn_kernel, half - 1, relayed + [up_all, down_all], [block] * (half - 1), shape, 2
    )
    results = list(expert_call(home_kernel, 1, [hidden_next] + downs_next, [block], shape, 1))
    results += [
        advanced(rows, 4 * place_of(d, half))
        for d, rows in enumerate([*near, far, *late], 1)
    ]
    count = (half - 1) * capacity
    sums = combine_call(
        functools.partial(mix_kernel, count),
        [x_next, info_next] + results[: half + 1],
        [jax.ShapeDtypeStruct(x.shape, F32)]
        + [jax.ShapeDtypeStruct((tok_rows, count), BF16)] * 2,
        (half + 1) * capacity,
    )
    (out,) = combine_call(
        last_kernel, [*sums, *results[half + 1 :]], [jax.ShapeDtypeStruct(x.shape, BF16)], count
    )
    return out[None]


def solution(mesh):
    in_specs = (
        P("section", "expert", None),
        P("section", None),
        P("section", None, "expert"),
        P("section", "expert", None),
        P(None, "section", "expert", None),
        P(None, "section", "expert", None),
    )
    out_specs = P("section", "expert", None)
    return jax.shard_map(step, mesh=mesh, in_specs=in_specs, out_specs=out_specs, check_vma=False)
```

```python
import functools

import jax
import jax.numpy as jnp
from jax import lax
from jax.experimental import pallas as pl
from jax.experimental.pallas import tpu as pltpu
from jax.sharding import PartitionSpec as P


VMEM = pl.BlockSpec(memory_space=pltpu.VMEM)
ANY = pl.BlockSpec(memory_space=pl.ANY)
VMEM_LIMIT = 32 * 2**20
BF16, F32 = jnp.bfloat16, jnp.float32


def exchanged(value, distance):
    count = lax.axis_size("expert")
    return lax.ppermute(value, "expert", [(i, i ^ distance) for i in range(count)])


def advanced(value, distance):
    sections, count = lax.axis_size("section"), lax.axis_size("expert")
    pairs = [
        (s * count + i, (s + 1) % sections * count + (i ^ distance))
        for s in range(sections)
        for i in range(count)
    ]
    return lax.ppermute(value, ("section", "expert"), pairs)


def place_of(distance, half):
    return distance + (distance >= half) * (3 * half - 1 - 2 * distance)


def use_of(place, half):
    near = (place > 0) & (place < half)
    return jnp.where(place == half, 1, jnp.where(near, place + 1, place))


def sort_kernel(blocks, capacity, with_info, x_ref, gain_ref, routes_ref, *refs):
    out_refs = refs[-blocks:]
    rows = x_ref.shape[0]
    own = lax.axis_index("expert") // 4
    r0, r1 = routes_ref[0:1, :], routes_ref[1:2, :]
    ids = lax.broadcasted_iota(jnp.int32, (max(2 * blocks, 8), rows), 0)
    named = jnp.where((ids == r0) | (ids == r1), 1.0, 0.0)
    before = lax.broadcasted_iota(jnp.int32, (rows, rows), 0) < lax.broadcasted_iota(
        jnp.int32, (rows, rows), 1
    )
    place = jnp.dot(
        named.astype(BF16), jnp.where(before, 1.0, 0.0).astype(BF16), preferred_element_type=F32
    )
    p0 = jnp.sum(jnp.where(ids == r0, place, 0.0), axis=0, keepdims=True)
    p1 = jnp.sum(jnp.where(ids == r1, place, 0.0), axis=0, keepdims=True)
    b0, b1 = place_of(r0 ^ own, blocks), place_of(r1 ^ own, blocks)
    p0, p1 = p0.astype(jnp.int32), p1.astype(jnp.int32)
    t0, t1 = b0 * capacity + p0, b1 * capacity + p1
    if with_info:
        gates_ref, info_ref = refs[:2]
        info_ref[0:1, :] = (use_of(b0, blocks) * capacity + p0).astype(F32)
        info_ref[1:2, :] = (use_of(b1, blocks) * capacity + p1).astype(F32)
        info_ref[2:4, :] = gates_ref[...]
        info_ref[4:8, :] = jnp.zeros((4, rows), F32)
    slots = lax.broadcasted_iota(jnp.int32, (blocks * capacity, rows), 0)
    chosen = jnp.where((slots == t0) | (slots == t1), 1.0, 0.0).astype(BF16)
    values = x_ref[...].astype(F32)
    scale = lax.rsqrt(jnp.mean(values * values, axis=-1, keepdims=True) + 1e-05)
    normed = (values * scale * gain_ref[...]).astype(BF16)
    sent = jnp.dot(chosen, normed, preferred_element_type=F32)
    for d, out_ref in enumerate(out_refs):
        out_ref[...] = sent[d * capacity : (d + 1) * capacity].astype(BF16)


def sort(x, gain, routes, gates, blocks, capacity):
    rows, width = x.shape
    with_info = gates is not None
    out_shape = [jax.ShapeDtypeStruct((8, rows), F32)] if with_info else []
    out_shape += [jax.ShapeDtypeStruct((capacity, width), BF16)] * blocks
    inputs = (x, gain, routes) + ((gates,) if with_info else ())
    return pl.pallas_call(
        functools.partial(sort_kernel, blocks, capacity, with_info),
        out_shape=out_shape,
        in_specs=[VMEM] * len(inputs),
        out_specs=[VMEM] * len(out_shape),
        cost_estimate=pl.CostEstimate(
            flops=2 * blocks * capacity * rows * width,
            bytes_accessed=2 * width * (rows + blocks * capacity),
            transcendentals=0,
        ),
        compiler_params=pltpu.CompilerParams(vmem_limit_bytes=VMEM_LIMIT),
        name="sort",
    )(*inputs)


def joined(sources, target, sems):
    size = sources[0].shape[0]
    copies = [
        pltpu.make_async_copy(src, target.at[pl.ds(i * size, size)], sems.at[i])
        for i, src in enumerate(sources)
    ]
    for copy in copies:
        copy.start()

    def read():
        for copy in copies:
            copy.wait()
        return target[...]

    return read


def hidden_of(row_refs, up):
    rows = jnp.concatenate([ref[...].astype(F32) for ref in row_refs], axis=0).astype(BF16)
    hidden = lax.dot_general(rows, up, (((1,), (1,)), ((), ())), preferred_element_type=F32)
    return jax.nn.gelu(hidden)


def outputs_of(hidden, down, out_refs):
    out = jnp.dot(hidden, down, preferred_element_type=F32)
    capacity = out_refs[0].shape[0]
    for d, out_ref in enumerate(out_refs):
        out_ref[...] = out[d * capacity : (d + 1) * capacity].astype(BF16)


def up_kernel(groups, *refs):
    own_ref, near_ref, up_ref, sems = refs[groups + 4 :]
    read = joined(refs[groups : groups + 4], up_ref, sems)
    hidden = hidden_of(refs[:groups], read())
    capacity = own_ref.shape[0]
    own_ref[...] = hidden[:capacity].astype(BF16)
    near_ref[...] = hidden[capacity:].astype(BF16)


def rise_kernel(groups, *refs):
    refs[-1][...] = hidden_of(refs[:groups], refs[groups][...]).astype(BF16)


def fall_kernel(groups, hidden_ref, *refs):
    *out_refs, down_ref, sems = refs[4:]
    outputs_of(hidden_ref[...], joined(refs[:4], down_ref, sems)(), out_refs)


def down_kernel(groups, hidden_ref, down_ref, *out_refs):
    outputs_of(hidden_ref[...], down_ref[...], out_refs)


def ffn_kernel(groups, *refs):
    up_ref, down_ref = refs[groups : groups + 2]
    hidden = hidden_of(refs[:groups], up_ref[...]).astype(BF16)
    outputs_of(hidden, down_ref[...], refs[groups + 2 :])


def home_kernel(groups, hidden_ref, *refs):
    *down_refs, out_ref = refs
    size = down_refs[0].shape[0]
    hidden = hidden_ref[...]
    out_ref[...] = sum(
        jnp.dot(hidden[:, i * size : (i + 1) * size], ref[...], preferred_element_type=F32)
        for i, ref in enumerate(down_refs)
    ).astype(BF16)


def expert_call(kernel, groups, inputs, outs, shape, products):
    (capacity, width), units = shape
    rows = groups * capacity
    return pl.pallas_call(
        functools.partial(kernel, groups),
        out_shape=[jax.ShapeDtypeStruct(shape, BF16) for shape in outs],
        in_specs=[VMEM] * len(inputs),
        out_specs=[VMEM] * len(outs),
        scratch_shapes=[pltpu.SemaphoreType.DMA((4,))] if kernel in (up_kernel, fall_kernel) else [],
        cost_estimate=pl.CostEstimate(
            flops=2 * products * rows * units * width,
            bytes_accessed=2 * products * width * (rows + units),
            transcendentals=rows * units,
        ),
        compiler_params=pltpu.CompilerParams(vmem_limit_bytes=VMEM_LIMIT),
    )(*inputs)


def slot_weights(info, first, count, dtype):
    slots = first + lax.broadcasted_iota(jnp.int32, (info.shape[0], count), 1)
    return sum(
        jnp.where(slots == info[:, k : k + 1].astype(jnp.int32), info[:, k + 2 : k + 3], 0.0)
        for k in range(2)
    ).astype(dtype)


def parts_of(weights):
    high = weights.astype(BF16)
    return high, (weights - high.astype(F32)).astype(BF16)


def taken(high, low, results):
    return jnp.dot(high, results, preferred_element_type=F32) + jnp.dot(
        low, results, preferred_element_type=F32
    )


def mix_kernel(late, x_ref, info_ref, *refs):
    result_refs, (sum_ref, high_ref, low_ref) = refs[:-3], refs[-3:]
    info = jnp.transpose(info_ref[...])
    results = jnp.concatenate([ref[...].astype(F32) for ref in result_refs], axis=0).astype(BF16)
    count = results.shape[0]
    high, low = parts_of(slot_weights(info, 0, count, F32))
    sum_ref[...] = x_ref[...].astype(F32) + taken(high, low, results)
    high_ref[...], low_ref[...] = parts_of(slot_weights(info, count, late, F32))


def last_kernel(sum_ref, high_ref, low_ref, *refs):
    *result_refs, out_ref, held, sems = refs
    high, low = high_ref[...], low_ref[...]
    pieces = sems.shape[0]
    width = out_ref.shape[1] // pieces
    copies = []
    for i in range(pieces):
        columns = pl.ds(i * width, width)
        results = [ref[:, columns].astype(F32) for ref in result_refs]
        results = jnp.concatenate(results, axis=0).astype(BF16)
        held[:, columns] = (sum_ref[:, columns] + taken(high, low, results)).astype(BF16)
        copies.append(pltpu.make_async_copy(held.at[:, columns], out_ref.at[:, columns], sems.at[i]))
        copies[-1].start()
    for copy in copies:
        copy.wait()


def combine_call(kernel, inputs, out_shape, slots, scratch=()):
    rows, width = inputs[0].shape
    return pl.pallas_call(
        kernel,
        out_shape=out_shape,
        in_specs=[VMEM] * len(inputs),
        out_specs=[ANY if scratch else VMEM] * len(out_shape),
        scratch_shapes=list(scratch),
        cost_estimate=pl.CostEstimate(
            flops=4 * rows * slots * width,
            bytes_accessed=2 * width * (3 * rows + slots),
            transcendentals=0,
        ),
        compiler_params=pltpu.CompilerParams(vmem_limit_bytes=VMEM_LIMIT),
    )(*inputs)


def step(carried, norm_gain, w_up, w_down, routes, gate_weights):
    half = lax.axis_size("expert") // 8
    x, routes_now = carried[0], routes[0, 0].T
    tok_rows, width = x.shape
    capacity = min(tok_rows, 4 * ((5 * tok_rows + 16 * half - 1) // (16 * half)))
    block = (capacity, width)
    up, down = w_up[0].T, w_down[0]
    units = (4 * up.shape[0], width)
    shape = (block, units[0])

    far_x = exchanged(x, 4 * (2 * half - 1))
    far_routes = exchanged(routes_now, 4 * (2 * half - 1))
    up_far, down_far = exchanged(up, 2), exchanged(down, 2)
    info, *own = sort(x, norm_gain, routes_now, gate_weights[0, 0].T, half, capacity)
    near = own[:1] + [exchanged(own[d], 4 * d) for d in range(1, half)]
    up_near, down_near = exchanged(up, 1), exchanged(down, 1)
    x_next, info_next = advanced(x, 0), advanced(info, 0)
    down_next = advanced(down, 0)
    down_next_far = exchanged(down_next, 2)
    downs_next = [down_next, exchanged(down_next, 1)]
    downs_next += [down_next_far, exchanged(down_next_far, 1)]
    ups = [up, up_near, up_far, exchanged(up_far, 1)]
    downs = [down, down_near, down_far, exchanged(down_far, 1)]
    hidden_own, hidden, up_all = expert_call(
        up_kernel,
        half,
        near + ups,
        [(capacity, units[0]), ((half - 1) * capacity, units[0]), units],
        shape,
        1,
    )
    hidden_next = advanced(hidden_own, 0)
    far, *relayed = sort(far_x, norm_gain, far_routes, None, half, capacity)
    relayed = [exchanged(rows, 4 * (d + 1)) for d, rows in enumerate(relayed)]
    (rise,) = expert_call(rise_kernel, 1, [far, up_all], [(capacity, units[0])], shape, 1)
    far, down_all = expert_call(fall_kernel, 1, [rise, *downs], [block, units], shape, 1)
    near = expert_call(down_kernel, half - 1, [hidden, down_all], [block] * (half - 1), shape, 1)
    late = expert_call(
        ffn_kernel, half - 1, relayed + [up_all, down_all], [block] * (half - 1), shape, 2
    )
    results = list(expert_call(home_kernel, 1, [hidden_next] + downs_next, [block], shape, 1))
    results += [
        advanced(rows, 4 * place_of(d, half))
        for d, rows in enumerate([*near, far, *late], 1)
    ]
    results = [results[0], results[half], *results[1:half], *results[half + 1 :]]
    count = (len(results) - 2) * capacity
    sums = combine_call(
        functools.partial(mix_kernel, count),
        [x_next, info_next] + results[:2],
        [jax.ShapeDtypeStruct(x.shape, F32)]
        + [jax.ShapeDtypeStruct((tok_rows, count), BF16)] * 2,
        2 * capacity,
    )
    (out,) = combine_call(
        last_kernel,
        [*sums, *results[2:]],
        [jax.ShapeDtypeStruct(x.shape, BF16)],
        count,
        [pltpu.VMEM(x.shape, BF16), pltpu.SemaphoreType.DMA((2,))],
    )
    return out[None]


def solution(mesh):
    in_specs = (
        P("section", "expert", None),
        P("section", None),
        P("section", None, "expert"),
        P("section", "expert", None),
        P(None, "section", "expert", None),
        P(None, "section", "expert", None),
    )
    out_specs = P("section", "expert", None)
    return jax.shard_map(step, mesh=mesh, in_specs=in_specs, out_specs=out_specs, check_vma=False)
```

```python
import functools

import jax
import jax.numpy as jnp
from jax import lax
from jax.experimental import pallas as pl
from jax.experimental.pallas import tpu as pltpu
from jax.sharding import PartitionSpec as P


VMEM = pl.BlockSpec(memory_space=pltpu.VMEM)
ANY = pl.BlockSpec(memory_space=pl.ANY)
VMEM_LIMIT = 32 * 2**20
BF16, F32 = jnp.bfloat16, jnp.float32


def exchanged(value, distance):
    count = lax.axis_size("expert")
    return lax.ppermute(value, "expert", [(i, i ^ distance) for i in range(count)])


def advanced(value, distance):
    sections, count = lax.axis_size("section"), lax.axis_size("expert")
    pairs = [
        (s * count + i, (s + 1) % sections * count + (i ^ distance))
        for s in range(sections)
        for i in range(count)
    ]
    return lax.ppermute(value, ("section", "expert"), pairs)


def place_of(distance, half):
    return distance + (distance >= half) * (3 * half - 1 - 2 * distance)


def use_of(place, half):
    near = (place > 0) & (place < half)
    return jnp.where(place == half, 1, jnp.where(near, place + 1, place))


def sort_kernel(blocks, capacity, with_info, x_ref, gain_ref, routes_ref, *refs):
    out_refs = refs[-blocks:]
    rows = x_ref.shape[0]
    own = lax.axis_index("expert") // 4
    r0, r1 = routes_ref[0:1, :], routes_ref[1:2, :]
    ids = lax.broadcasted_iota(jnp.int32, (max(2 * blocks, 8), rows), 0)
    named = jnp.where((ids == r0) | (ids == r1), 1.0, 0.0)
    before = lax.broadcasted_iota(jnp.int32, (rows, rows), 0) < lax.broadcasted_iota(
        jnp.int32, (rows, rows), 1
    )
    place = jnp.dot(
        named.astype(BF16), jnp.where(before, 1.0, 0.0).astype(BF16), preferred_element_type=F32
    )
    p0 = jnp.sum(jnp.where(ids == r0, place, 0.0), axis=0, keepdims=True)
    p1 = jnp.sum(jnp.where(ids == r1, place, 0.0), axis=0, keepdims=True)
    b0, b1 = place_of(r0 ^ own, blocks), place_of(r1 ^ own, blocks)
    p0, p1 = p0.astype(jnp.int32), p1.astype(jnp.int32)
    t0, t1 = b0 * capacity + p0, b1 * capacity + p1
    if with_info:
        gates_ref, info_ref = refs[:2]
        info_ref[0:1, :] = (use_of(b0, blocks) * capacity + p0).astype(F32)
        info_ref[1:2, :] = (use_of(b1, blocks) * capacity + p1).astype(F32)
        info_ref[2:4, :] = gates_ref[...]
        info_ref[4:8, :] = jnp.zeros((4, rows), F32)
    slots = lax.broadcasted_iota(jnp.int32, (blocks * capacity, rows), 0)
    chosen = jnp.where((slots == t0) | (slots == t1), 1.0, 0.0).astype(BF16)
    values = x_ref[...].astype(F32)
    scale = lax.rsqrt(jnp.mean(values * values, axis=-1, keepdims=True) + 1e-05)
    normed = (values * scale * gain_ref[...]).astype(BF16)
    sent = jnp.dot(chosen, normed, preferred_element_type=F32)
    for d, out_ref in enumerate(out_refs):
        out_ref[...] = sent[d * capacity : (d + 1) * capacity].astype(BF16)


def sort(x, gain, routes, gates, blocks, capacity):
    rows, width = x.shape
    with_info = gates is not None
    out_shape = [jax.ShapeDtypeStruct((8, rows), F32)] if with_info else []
    out_shape += [jax.ShapeDtypeStruct((capacity, width), BF16)] * blocks
    inputs = (x, gain, routes) + ((gates,) if with_info else ())
    return pl.pallas_call(
        functools.partial(sort_kernel, blocks, capacity, with_info),
        out_shape=out_shape,
        in_specs=[VMEM] * len(inputs),
        out_specs=[VMEM] * len(out_shape),
        cost_estimate=pl.CostEstimate(
            flops=2 * blocks * capacity * rows * width,
            bytes_accessed=2 * width * (rows + blocks * capacity),
            transcendentals=0,
        ),
        compiler_params=pltpu.CompilerParams(vmem_limit_bytes=VMEM_LIMIT),
        name="sort",
    )(*inputs)


def joined(sources, target, sems):
    size = sources[0].shape[0]
    copies = [
        pltpu.make_async_copy(src, target.at[pl.ds(i * size, size)], sems.at[i])
        for i, src in enumerate(sources)
    ]
    for copy in copies:
        copy.start()

    def read():
        for copy in copies:
            copy.wait()
        return target[...]

    return read


def hidden_of(row_refs, up):
    rows = jnp.concatenate([ref[...].astype(F32) for ref in row_refs], axis=0).astype(BF16)
    hidden = lax.dot_general(rows, up, (((1,), (1,)), ((), ())), preferred_element_type=F32)
    return jax.nn.gelu(hidden)


def outputs_of(hidden, down, out_refs):
    out = jnp.dot(hidden, down, preferred_element_type=F32)
    capacity = out_refs[0].shape[0]
    for d, out_ref in enumerate(out_refs):
        out_ref[...] = out[d * capacity : (d + 1) * capacity].astype(BF16)


def up_kernel(groups, *refs):
    own_ref, up_ref, sems = refs[groups + 4 :]
    read = joined(refs[groups : groups + 4], up_ref, sems)
    own_ref[...] = hidden_of(refs[:groups], read()).astype(BF16)


def rise_kernel(groups, *refs):
    refs[-1][...] = hidden_of(refs[:groups], refs[groups][...]).astype(BF16)


def fall_kernel(groups, hidden_ref, *refs):
    *out_refs, down_ref, sems = refs[4:]
    outputs_of(hidden_ref[...], joined(refs[:4], down_ref, sems)(), out_refs)


def ffn_kernel(groups, *refs):
    up_ref, down_ref = refs[groups : groups + 2]
    hidden = hidden_of(refs[:groups], up_ref[...]).astype(BF16)
    outputs_of(hidden, down_ref[...], refs[groups + 2 :])


def home_kernel(groups, hidden_ref, *refs):
    *down_refs, out_ref = refs
    size = down_refs[0].shape[0]
    hidden = hidden_ref[...]
    out_ref[...] = sum(
        jnp.dot(hidden[:, i * size : (i + 1) * size], ref[...], preferred_element_type=F32)
        for i, ref in enumerate(down_refs)
    ).astype(BF16)


def expert_call(kernel, groups, inputs, outs, shape, products):
    (capacity, width), units = shape
    rows = groups * capacity
    return pl.pallas_call(
        functools.partial(kernel, groups),
        out_shape=[jax.ShapeDtypeStruct(shape, BF16) for shape in outs],
        in_specs=[VMEM] * len(inputs),
        out_specs=[VMEM] * len(outs),
        scratch_shapes=[pltpu.SemaphoreType.DMA((4,))] if kernel in (up_kernel, fall_kernel) else [],
        cost_estimate=pl.CostEstimate(
            flops=2 * products * rows * units * width,
            bytes_accessed=2 * products * width * (rows + units),
            transcendentals=rows * units,
        ),
        compiler_params=pltpu.CompilerParams(vmem_limit_bytes=VMEM_LIMIT),
    )(*inputs)


def slot_weights(info, first, count, dtype):
    slots = first + lax.broadcasted_iota(jnp.int32, (info.shape[0], count), 1)
    return sum(
        jnp.where(slots == info[:, k : k + 1].astype(jnp.int32), info[:, k + 2 : k + 3], 0.0)
        for k in range(2)
    ).astype(dtype)


def parts_of(weights):
    high = weights.astype(BF16)
    return high, (weights - high.astype(F32)).astype(BF16)


def taken(high, low, results):
    rows = high.shape[0]
    both = jnp.dot(jnp.concatenate([high, low], axis=0), results, preferred_element_type=F32)
    return both[:rows] + both[rows:]


def mix_kernel(late, x_ref, info_ref, *refs):
    result_refs, (sum_ref, high_ref, low_ref) = refs[:-3], refs[-3:]
    info = jnp.transpose(info_ref[...])
    results = jnp.concatenate([ref[...].astype(F32) for ref in result_refs], axis=0).astype(BF16)
    count = results.shape[0]
    high, low = parts_of(slot_weights(info, 0, count, F32))
    sum_ref[...] = x_ref[...].astype(F32) + taken(high, low, results)
    high_ref[...], low_ref[...] = parts_of(slot_weights(info, count, late, F32))


def last_kernel(sum_ref, high_ref, low_ref, *refs):
    *result_refs, out_ref, held, sems = refs
    high, low = high_ref[...], low_ref[...]
    pieces = sems.shape[0]
    width = out_ref.shape[1] // pieces
    copies = []
    for i in range(pieces):
        columns = pl.ds(i * width, width)
        results = [ref[:, columns].astype(F32) for ref in result_refs]
        results = jnp.concatenate(results, axis=0).astype(BF16)
        held[:, columns] = (sum_ref[:, columns] + taken(high, low, results)).astype(BF16)
        copies.append(pltpu.make_async_copy(held.at[:, columns], out_ref.at[:, columns], sems.at[i]))
        copies[-1].start()
    for copy in copies:
        copy.wait()


def combine_call(kernel, inputs, out_shape, slots, scratch=()):
    rows, width = inputs[0].shape
    return pl.pallas_call(
        kernel,
        out_shape=out_shape,
        in_specs=[VMEM] * len(inputs),
        out_specs=[ANY if scratch else VMEM] * len(out_shape),
        scratch_shapes=list(scratch),
        cost_estimate=pl.CostEstimate(
            flops=4 * rows * slots * width,
            bytes_accessed=2 * width * (3 * rows + slots),
            transcendentals=0,
        ),
        compiler_params=pltpu.CompilerParams(vmem_limit_bytes=VMEM_LIMIT),
    )(*inputs)


def step(carried, norm_gain, w_up, w_down, routes, gate_weights):
    half = lax.axis_size("expert") // 8
    x, routes_now = carried[0], routes[0, 0].T
    tok_rows, width = x.shape
    capacity = min(tok_rows, 4 * ((5 * tok_rows + 16 * half - 1) // (16 * half)))
    block = (capacity, width)
    up, down = w_up[0].T, w_down[0]
    units = (4 * up.shape[0], width)
    shape = (block, units[0])

    far_x = exchanged(x, 4 * (2 * half - 1))
    far_routes = exchanged(routes_now, 4 * (2 * half - 1))
    up_far, down_far = exchanged(up, 2), exchanged(down, 2)
    info, *own = sort(x, norm_gain, routes_now, gate_weights[0, 0].T, half, capacity)
    near = own[:1] + [exchanged(own[d], 4 * d) for d in range(1, half)]
    up_near, down_near = exchanged(up, 1), exchanged(down, 1)
    x_next, info_next = advanced(x, 0), advanced(info, 0)
    down_next = advanced(down, 0)
    down_next_far = exchanged(down_next, 2)
    downs_next = [down_next, exchanged(down_next, 1)]
    downs_next += [down_next_far, exchanged(down_next_far, 1)]
    ups = [up, up_near, up_far, exchanged(up_far, 1)]
    downs = [down, down_near, down_far, exchanged(down_far, 1)]
    hidden_own, up_all = expert_call(
        up_kernel, 1, near[:1] + ups, [(capacity, units[0]), units], shape, 1
    )
    hidden_next = advanced(hidden_own, 0)
    far, *relayed = sort(far_x, norm_gain, far_routes, None, half, capacity)
    relayed = [exchanged(rows, 4 * (d + 1)) for d, rows in enumerate(relayed)]
    (rise,) = expert_call(rise_kernel, 1, [far, up_all], [(capacity, units[0])], shape, 1)
    far, down_all = expert_call(fall_kernel, 1, [rise, *downs], [block, units], shape, 1)
    near = expert_call(
        ffn_kernel, half - 1, near[1:] + [up_all, down_all], [block] * (half - 1), shape, 2
    )
    late = expert_call(
        ffn_kernel, half - 1, relayed + [up_all, down_all], [block] * (half - 1), shape, 2
    )
    results = list(expert_call(home_kernel, 1, [hidden_next] + downs_next, [block], shape, 1))
    results += [
        advanced(rows, 4 * place_of(d, half))
        for d, rows in enumerate([*near, far, *late], 1)
    ]
    results = [results[0], results[half], *results[1:half], *results[half + 1 :]]
    count = (len(results) - 2) * capacity
    sums = combine_call(
        functools.partial(mix_kernel, count),
        [x_next, info_next] + results[:2],
        [jax.ShapeDtypeStruct(x.shape, F32)]
        + [jax.ShapeDtypeStruct((tok_rows, count), BF16)] * 2,
        2 * capacity,
    )
    (out,) = combine_call(
        last_kernel,
        [*sums, *results[2:]],
        [jax.ShapeDtypeStruct(x.shape, BF16)],
        count,
        [pltpu.VMEM(x.shape, BF16), pltpu.SemaphoreType.DMA((4,))],
    )
    return out[None]


def solution(mesh):
    in_specs = (
        P("section", "expert", None),
        P("section", None),
        P("section", None, "expert"),
        P("section", "expert", None),
        P(None, "section", "expert", None),
        P(None, "section", "expert", None),
    )
    out_specs = P("section", "expert", None)
    return jax.shard_map(step, mesh=mesh, in_specs=in_specs, out_specs=out_specs, check_vma=False)
```
